32 devices in a mesh: groups: 2 (over y), row: 16 (over z, x, core).
Axes of the slice: x: 2, y: 2, z: 4, core: 2. Of those that a mesh axis runs over, the one named last changes fastest.
Arguments:
- late_grads: bfloat16 [64, 16, 4, 4096], P(('groups', 'row')), parts along dimension 0, may hold values from -6 to 6
- projections: bfloat16 [4096, 256], replicated, may hold values from -0.09375 to 0.09375
- recent_sketches: bfloat16 [8192, 8192], P(('groups', 'row')), parts along dimension 0, may hold values from -6 to 6
Outputs:
- reweighted: bfloat16 [64, 8192], P(('groups', 'row')), parts along dimension 0
The draws below stay inside these ranges and needn't reach their ends.
There are 2 independent parts, one for each index of `groups`. The reference program is written for one: setup_inputs(seed, part) draws one part's arguments, and reference() takes and returns one part's arrays. A program takes and returns all parts, laid end to end along the dimension named above; an argument that names none is the same for every part. Nothing has to cross between parts.
All inputs are finite; a program needn't handle non-finite values.
Results may differ from the reference program's by a relative error of at most 0.0076.
Values may be sent and summed in bfloat16 or wider, within the bound.
A program may use at most 64 MiB of HBM per device.

```python
import jax
import jax.numpy as jnp

D = 4096
RANK = 64
ITEMS = 16
K = 8192
L_TOT = 32
R_TOT = 4096


def steps_of(key, shape, pieces, smallest, largest):
    def one(position, blocks):
        draws = jax.random.uniform(jax.random.fold_in(jax.random.fold_in(key, 6), position), (blocks,), jnp.float32, smallest / len(pieces), largest / len(pieces))
        return jnp.repeat(jnp.exp(draws), shape[position] // blocks).reshape((-1,) + (1,) * (len(shape) - position - 1))

    gain = one(*pieces[0])
    for cut in pieces[1:]:
        gain = gain * one(*cut)
    return gain


def bell_draw(own_key, shape, width, bound, cuts=(), held_as=jnp.bfloat16):
    array = width * jax.random.normal(own_key, shape, jnp.float32)
    if cuts:
        array = array * steps_of(own_key, shape, cuts, -0.22, 0.18)
    return jnp.clip(array, -bound, bound).astype(held_as)


def setup_inputs(seed: int = 0, part: int = 0) -> dict:
    seeds = jax.random.split(jax.random.key(seed), 4)
    part_splits = jax.random.split(jax.random.fold_in(seeds[3], part), 4)
    late_grads = bell_draw(part_splits[0], (L_TOT, ITEMS, 4, D), 1.0, 6.0, ((0, 16),))
    projections = bell_draw(seeds[1], (D, 4 * RANK), D ** -0.5, 0.09375)
    recent_sketches = bell_draw(part_splits[2], (R_TOT, K), 1.0, 6.0, ((0, 16),))
    return dict(late_grads=late_grads, projections=projections, recent_sketches=recent_sketches)


def build_sketch(factors):
    count = factors.shape[0]
    parts = factors.reshape(count, ITEMS, 4, RANK)
    blocks = []
    for layer in range(2):
        left = parts[:, :, 2 * layer + 1, :].astype(jnp.float32)
        right = parts[:, :, 2 * layer, :].astype(jnp.float32)
        outer = jnp.einsum('eti,etj->eij', left, right)
        blocks.append(outer.reshape(count, RANK * RANK))
    joined = jnp.concatenate(blocks, axis=1) / jnp.sqrt(jnp.float32(ITEMS))
    return joined.astype(jnp.bfloat16)

def reference(late_grads, projections, recent_sketches):
    proj_blocks = projections.reshape(D, 4, RANK).astype(jnp.float32)
    factors = jnp.einsum('etkd,dkr->etkr', late_grads.astype(jnp.float32), proj_blocks)
    factors = factors.astype(jnp.bfloat16).reshape(L_TOT, ITEMS, 4 * RANK)
    late_sketch = build_sketch(factors)
    similarity = jnp.dot(late_sketch, recent_sketches.T, preferred_element_type=jnp.float32) / jnp.sqrt(jnp.float32(K))
    weights = jnp.tanh(similarity).astype(jnp.bfloat16)
    summed = jnp.dot(weights, recent_sketches, preferred_element_type=jnp.float32)
    return (summed / jnp.sqrt(jnp.float32(R_TOT))).astype(jnp.bfloat16)
```

```python
import functools
import math

import jax
import jax.numpy as jnp
from jax import lax
from jax.experimental import pallas as pl
from jax.experimental.pallas import tpu as pltpu
from jax.sharding import PartitionSpec as P

GROUP = 8
CHUNKS = 4
MESH = pl.DeviceIdType.MESH


def kernel(
    dims, items, rank, total_recent,
    late_hbm, proj_hbm, recent_hbm, out_ref,
    late, proj, recent, gath, wmask, tf, tb, r1, s1f, s1b, r2, s2f, s2b, r3,
    load_sem, g_send, g_recv, c_send, c_recv, x_send, x_recv, z_send, z_recv,
):
    nz, nx, nc = dims
    width = recent_hbm.shape[1]
    part = width // GROUP
    local_recent = recent_hbm.shape[0]
    slab = gath.shape[3]
    examples = slab // GROUP
    n = nz * nx * nc
    me = lax.axis_index("row")
    mc = lax.rem(me, nc)
    mx = lax.rem(lax.div(me, nc), nx)
    mz = lax.div(me, nc * nx)
    oc = 1 - mc

    def flat(z, x, c):
        return {"row": (z * nx + x) * nc + c}

    load_late = pltpu.make_async_copy(late_hbm, late, load_sem.at[0])
    load_proj = pltpu.make_async_copy(proj_hbm, proj, load_sem.at[1])
    load_late.start()
    load_proj.start()
    load_recent = []
    for q in range(GROUP):
        copy = pltpu.make_async_copy(
            recent_hbm.at[:, pl.ds(q * part, part)],
            recent.at[pl.ds(q * local_recent, local_recent), :],
            load_sem.at[2 + q],
        )
        copy.start()
        load_recent.append(copy)

    peers = [(mz, mx, oc)]
    peers += [(mz, lax.rem(mx + d, nx), mc) for d in range(1, nx)]
    peers += [(lax.rem(mz + d, nz), mx, mc) for d in range(1, nz)]
    barrier = pltpu.get_barrier_semaphore()
    for z, x, c in peers:
        pl.semaphore_signal(barrier, inc=1, device_id=flat(z, x, c), device_id_type=MESH)

    def onehot(shape, expr):
        r = lax.broadcasted_iota(jnp.int32, shape, 0)
        c = lax.broadcasted_iota(jnp.int32, shape, 1)
        return jnp.where(expr(r, c), 1.0, 0.0).astype(jnp.bfloat16)

    pairs = examples * items
    pick = onehot((pairs, 4 * pairs), lambda r, c: r == lax.shift_right_logical(c, 2))
    spread = onehot((rank, part), lambda r, c: r == lax.rem(c, rank))
    repeat = onehot((rank, rank * rank), lambda r, c: r == lax.div(c, rank))

    load_late.wait()
    load_proj.wait()
    rows = late[...].reshape(4 * pairs, late.shape[2])
    full = jnp.dot(rows, proj[...], preferred_element_type=jnp.float32)
    kind = lax.rem(lax.broadcasted_iota(jnp.int32, full.shape, 0), 4)
    block = lax.div(lax.broadcasted_iota(jnp.int32, full.shape, 1), rank)
    full = jnp.where(kind == block, full, 0.0).astype(jnp.bfloat16)
    factors = jnp.dot(pick, full, preferred_element_type=jnp.float32)
    sketch = jnp.zeros((slab, part), jnp.float32)
    row = lax.broadcasted_iota(jnp.int32, (slab, part), 0)
    quarter = GROUP // 2
    for layer in range(2):
        right = factors[:, 2 * layer * rank : (2 * layer + 1) * rank].astype(jnp.bfloat16)
        left = factors[:, (2 * layer + 1) * rank : (2 * layer + 2) * rank].astype(jnp.bfloat16)
        tiled = jnp.dot(right, spread, preferred_element_type=jnp.float32)
        for q in range(quarter):
            wide = jnp.dot(
                left, repeat[:, q * part : (q + 1) * part], preferred_element_type=jnp.float32
            )
            outer = wide * tiled
            for e in range(examples):
                total = jnp.sum(outer[e * items : (e + 1) * items], axis=0, keepdims=True)
                at = e * GROUP + layer * quarter + q
                sketch = jnp.where(row == at, total, sketch)
    gath[mz, mx, mc] = (sketch * (1.0 / math.sqrt(items))).astype(jnp.bfloat16)

    pl.semaphore_wait(barrier, len(peers))

    sent = []

    def forward(z, x, c, to, slot):
        copy = pltpu.make_async_remote_copy(
            src_ref=gath.at[z, x, c], dst_ref=gath.at[z, x, c],
            send_sem=g_send.at[slot], recv_sem=g_recv.at[z, x, c],
            device_id=flat(*to), device_id_type=MESH,
        )
        copy.start()
        sent.append(copy)

    def arrived(z, x, c):
        pltpu.make_async_remote_copy(
            src_ref=gath.at[z, x, c], dst_ref=gath.at[z, x, c],
            send_sem=g_send.at[0], recv_sem=g_recv.at[z, x, c],
            device_id=flat(mz, mx, oc), device_id_type=MESH,
        ).wait_recv()

    slot = 0
    for d in range(1, nz):
        forward(mz, mx, mc, (lax.rem(mz + d, nz), mx, mc), slot)
        slot += 1
    for dz in range(nz):
        z = lax.rem(mz + nz - dz, nz)
        if dz:
            arrived(z, mx, mc)
        for d in range(1, nx):
            forward(z, mx, mc, (mz, lax.rem(mx + d, nx), mc), slot)
            slot += 1
        forward(z, mx, mc, (mz, mx, oc), slot)
        slot += 1
    for dz in range(nz):
        z = lax.rem(mz + nz - dz, nz)
        for d in range(1, nx):
            x = lax.rem(mx + nx - d, nx)
            arrived(z, x, mc)
            forward(z, x, mc, (mz, mx, oc), slot)
            slot += 1
    for copy in load_recent:
        copy.wait()
    for dz in range(nz):
        z = lax.rem(mz + nz - dz, nz)
        for d in range(nx):
            arrived(z, lax.rem(mx + nx - d, nx), oc)

    zb = max(1, min(nz, 256 // (nx * nc * slab)))
    rb = zb * nx * nc * slab

    def similar(b):
        base = b * zb
        every = gath[pl.ds(base, zb)].reshape(rb, part)
        group = lax.rem(lax.broadcasted_iota(jnp.int32, (rb, local_recent), 0), GROUP)
        acc = jnp.zeros((rb, local_recent), jnp.float32)
        for q in range(GROUP):
            term = lax.dot_general(
                every, recent[q * local_recent : (q + 1) * local_recent, :],
                (((1,), (1,)), ((), ())), preferred_element_type=jnp.float32,
            )
            acc = jnp.where(group == q, term, acc)
        acc = acc.reshape(rb // GROUP, GROUP, local_recent)
        sim = jnp.sum(acc, axis=1, keepdims=True) * (1.0 / math.sqrt(width))
        weights = jnp.broadcast_to(jnp.tanh(sim), acc.shape).reshape(rb, local_recent)
        for q in range(GROUP):
            wmask[pl.ds(b * rb, rb), q * local_recent : (q + 1) * local_recent] = jnp.where(
                group == q, weights, 0.0
            ).astype(jnp.bfloat16)

    def each_block(body):
        if nz == zb:
            body(0)
        else:
            lax.fori_loop(0, nz // zb, lambda b, c: (body(b), c)[1], 0)

    each_block(similar)

    cw = part // CHUNKS
    copies = []

    def start(src, dst, ss, rs, to):
        copy = pltpu.make_async_remote_copy(
            src_ref=src, dst_ref=dst, send_sem=ss, recv_sem=rs,
            device_id=flat(*to), device_id_type=MESH,
        )
        copy.start()
        copies.append(copy)
        return copy

    core_copies, x_copies, z_copies = {}, {}, {}

    def stage_core(k):
        cols = pl.ds(k * cw, cw)

        def body(b):
            term = jnp.dot(
                wmask[pl.ds(b * rb, rb), :], recent[:, k * cw : (k + 1) * cw],
                preferred_element_type=jnp.float32,
            ).reshape(zb, nx, nc, slab, cw)
            tf[pl.ds(b * zb, zb), :, :, :, cols] = term
            tb[pl.ds(b * zb, zb), :, :, :, cols] = term.astype(jnp.bfloat16)

        each_block(body)
        core_copies[k] = start(
            tb.at[:, :, oc, :, cols], r1.at[:, :, :, cols],
            c_send.at[k], c_recv.at[k], (mz, mx, oc),
        )

    def stage_x(k):
        cols = pl.ds(k * cw, cw)
        core_copies[k].wait_recv()
        for z in range(nz):
            for x in range(nx):
                total = tf[z, x, mc, :, cols] + r1[z, x, :, cols].astype(jnp.float32)
                s1f[z, x, :, cols] = total
                s1b[z, x, :, cols] = total.astype(jnp.bfloat16)
        for d in range(1, nx):
            x = lax.rem(mx + d, nx)
            x_copies[k, d] = start(
                s1b.at[:, x, :, cols], r2.at[d - 1, :, :, cols],
                x_send.at[k, d - 1], x_recv.at[k, d - 1], (mz, x, mc),
            )

    def stage_z(k):
        cols = pl.ds(k * cw, cw)
        for d in range(1, nx):
            x_copies[k, d].wait_recv()
        for z in range(nz):
            total = s1f[z, mx, :, cols]
            for d in range(1, nx):
                total = total + r2[d - 1, z, :, cols].astype(jnp.float32)
            s2f[z, :, cols] = total
            s2b[z, :, cols] = total.astype(jnp.bfloat16)
        for d in range(1, nz):
            z = lax.rem(mz + d, nz)
            z_copies[k, d] = start(
                s2b.at[z, :, cols], r3.at[d - 1, :, cols],
                z_send.at[k, d - 1], z_recv.at[k, d - 1], (z, mx, mc),
            )

    def finish(k):
        cols = pl.ds(k * cw, cw)
        total = s2f[mz, :, cols]
        for d in range(1, nz):
            z_copies[k, d].wait_recv()
            total = total + r3[d - 1, :, cols].astype(jnp.float32)
        out_ref[:, cols] = (total * (1.0 / math.sqrt(total_recent))).astype(jnp.bfloat16)

    stages = (stage_core, stage_x, stage_z, finish)
    for step in range(CHUNKS + len(stages) - 1):
        for index, stage in enumerate(stages):
            if 0 <= step - index < CHUNKS:
                stage(step - index)
    for copy in sent + copies:
        copy.wait_send()


def per_device(dims, late_grads, projections, recent_sketches):
    nz, nx, nc = dims
    local_rows, items, kinds, width_in = late_grads.shape
    rank = projections.shape[1] // 4
    local_recent, width = recent_sketches.shape
    n = nz * nx * nc
    slab, part = local_rows * GROUP, width // GROUP
    bf16, f32 = jnp.bfloat16, jnp.float32
    dma = pltpu.SemaphoreType.DMA
    sends = (nz - 1) + nz * nx + nz * (nx - 1)
    out = pl.pallas_call(
        functools.partial(kernel, dims, items, rank, local_recent * n),
        out_shape=jax.ShapeDtypeStruct((slab, part), bf16),
        in_specs=[pl.BlockSpec(memory_space=pl.ANY)] * 3,
        out_specs=pl.BlockSpec(memory_space=pltpu.VMEM),
        scratch_shapes=[
            pltpu.VMEM((local_rows * items, kinds, width_in), bf16),
            pltpu.VMEM(projections.shape, bf16),
            pltpu.VMEM((GROUP * local_recent, part), bf16),
            pltpu.VMEM((nz, nx, nc, slab, part), bf16),
            pltpu.VMEM((n * slab, GROUP * local_recent), bf16),
            pltpu.VMEM((nz, nx, nc, slab, part), f32),
            pltpu.VMEM((nz, nx, nc, slab, part), bf16),
            pltpu.VMEM((nz, nx, slab, part), bf16),
            pltpu.VMEM((nz, nx, slab, part), f32),
            pltpu.VMEM((nz, nx, slab, part), bf16),
            pltpu.VMEM((nx - 1, nz, slab, part), bf16),
            pltpu.VMEM((nz, slab, part), f32),
            pltpu.VMEM((nz, slab, part), bf16),
            pltpu.VMEM((nz - 1, slab, part), bf16),
            dma((2 + GROUP,)),
            dma((sends + nz * nx,)),
            dma(dims),
            dma((CHUNKS,)),
            dma((CHUNKS,)),
            dma((CHUNKS, nx - 1)),
            dma((CHUNKS, nx - 1)),
            dma((CHUNKS, nz - 1)),
            dma((CHUNKS, nz - 1)),
        ],
        compiler_params=pltpu.CompilerParams(
            collective_id=0, has_side_effects=True, vmem_limit_bytes=60 * 1024 * 1024
        ),
    )(late_grads.reshape(local_rows * items, kinds, width_in), projections, recent_sketches)
    return out.reshape(local_rows, width)


def solution(mesh):
    n = mesh.shape["row"]
    nx = 4 if n >= 64 else 2
    dims = (n // (2 * nx), nx, 2)
    placed = (P(("groups", "row"), None, None, None), P(), P(("groups", "row"), None))
    return jax.shard_map(
        functools.partial(per_device, dims),
        mesh=mesh,
        in_specs=placed,
        out_specs=P(("groups", "row"), None),
        check_vma=False,
    )
```

```python
import functools
import math

import jax
import jax.numpy as jnp
from jax import lax
from jax.experimental import pallas as pl
from jax.experimental.pallas import tpu as pltpu
from jax.sharding import PartitionSpec as P

GROUP = 8
CHUNKS = 2
LOADS = 4
MESH = pl.DeviceIdType.MESH


def kernel(
    dims, items, rank, total_recent,
    late_hbm, proj_hbm, recent_hbm, out_ref,
    late, proj, recent, gath, wmask, tf, tb, r1, s1f, s1b, r2, s2f, s2b, r3,
    t1b, t2, t2f, t2b, t3,
    load_sem, g_send, g_recv, c_send, c_recv, x_send, x_recv, z_send, z_recv,
):
    nz, nx, nc = dims
    width = recent_hbm.shape[1]
    part = width // GROUP
    local_recent = recent_hbm.shape[0]
    slab = gath.shape[3]
    examples = slab // GROUP
    n = nz * nx * nc
    me = lax.axis_index("row")
    mc = lax.rem(me, nc)
    mx = lax.rem(lax.div(me, nc), nx)
    mz = lax.div(me, nc * nx)
    oc = 1 - mc

    def across(z, d):
        bit = 1
        while bit <= d:
            if d & bit:
                z = z + bit - 2 * bit * lax.rem(lax.div(z, bit), 2)
            bit *= 2
        return z

    def flat(z, x, c):
        return {"row": (z * nx + x) * nc + c}

    depth = late.shape[2] // LOADS
    load_inputs = []
    for i in range(LOADS):
        part_of = pl.ds(i * depth, depth)
        pair = (
            pltpu.make_async_copy(late_hbm.at[:, :, part_of], late.at[:, :, part_of], load_sem.at[GROUP + i]),
            pltpu.make_async_copy(proj_hbm.at[part_of], proj.at[part_of], load_sem.at[GROUP + LOADS + i]),
        )
        for copy in pair:
            copy.start()
        load_inputs.append(pair)

    peers = [(mz, mx, oc)]
    peers += [(mz, lax.rem(mx + d, nx), mc) for d in range(1, nx)]
    peers += [(across(mz, d), mx, mc) for d in range(1, nz)]
    barrier = pltpu.get_barrier_semaphore()
    for z, x, c in peers:
        pl.semaphore_signal(barrier, inc=1, device_id=flat(z, x, c), device_id_type=MESH)

    def onehot(shape, expr):
        r = lax.broadcasted_iota(jnp.int32, shape, 0)
        c = lax.broadcasted_iota(jnp.int32, shape, 1)
        return jnp.where(expr(r, c), 1.0, 0.0).astype(jnp.bfloat16)

    pairs = examples * items
    pick = onehot((pairs, 4 * pairs), lambda r, c: r == lax.shift_right_logical(c, 2))
    spread = onehot((rank, part), lambda r, c: r == lax.rem(c, rank))
    repeat = onehot((rank, rank * rank), lambda r, c: r == lax.div(c, rank))

    full = jnp.zeros((4 * pairs, 4 * rank), jnp.float32)
    for i, pair in enumerate(load_inputs):
        for copy in pair:
            copy.wait()
        rows = late[:, :, i * depth : (i + 1) * depth].reshape(4 * pairs, depth)
        full = full + jnp.dot(
            rows, proj[i * depth : (i + 1) * depth, :], preferred_element_type=jnp.float32
        )
    load_recent = []
    for q in range(GROUP):
        copy = pltpu.make_async_copy(
            recent_hbm.at[:, pl.ds(q * part, part)],
            recent.at[pl.ds(q * local_recent, local_recent), :],
            load_sem.at[q],
        )
        copy.start()
        load_recent.append(copy)
    kind = lax.rem(lax.broadcasted_iota(jnp.int32, full.shape, 0), 4)
    block = lax.div(lax.broadcasted_iota(jnp.int32, full.shape, 1), rank)
    full = jnp.where(kind == block, full, 0.0).astype(jnp.bfloat16)
    factors = jnp.dot(pick, full, preferred_element_type=jnp.float32)
    sketch = jnp.zeros((slab, part), jnp.float32)
    row = lax.broadcasted_iota(jnp.int32, (slab, part), 0)
    quarter = GROUP // 2
    for layer in range(2):
        right = factors[:, 2 * layer * rank : (2 * layer + 1) * rank].astype(jnp.bfloat16)
        left = factors[:, (2 * layer + 1) * rank : (2 * layer + 2) * rank].astype(jnp.bfloat16)
        tiled = jnp.dot(right, spread, preferred_element_type=jnp.float32)
        for q in range(quarter):
            wide = jnp.dot(
                left, repeat[:, q * part : (q + 1) * part], preferred_element_type=jnp.float32
            )
            outer = wide * tiled
            for e in range(examples):
                total = jnp.sum(outer[e * items : (e + 1) * items], axis=0, keepdims=True)
                at = e * GROUP + layer * quarter + q
                sketch = jnp.where(row == at, total, sketch)
    gath[mc, mx, mz] = (sketch * (1.0 / math.sqrt(items))).astype(jnp.bfloat16)

    pl.semaphore_wait(barrier, len(peers))

    sent = []

    def forward(z, x, c, to, slot):
        copy = pltpu.make_async_remote_copy(
            src_ref=gath.at[c, x, z], dst_ref=gath.at[c, x, z],
            send_sem=g_send.at[slot], recv_sem=g_recv.at[z, x, c],
            device_id=flat(*to), device_id_type=MESH,
        )
        copy.start()
        sent.append(copy)

    def arrived(z, x, c):
        pltpu.make_async_remote_copy(
            src_ref=gath.at[c, x, z], dst_ref=gath.at[c, x, z],
            send_sem=g_send.at[0], recv_sem=g_recv.at[z, x, c],
            device_id=flat(mz, mx, oc), device_id_type=MESH,
        ).wait_recv()

    slot = 0
    for d in range(1, nz):
        forward(mz, mx, mc, (across(mz, d), mx, mc), slot)
        slot += 1
    for dz in range(nz):
        z = across(mz, dz)
        if dz:
            arrived(z, mx, mc)
        for d in range(1, nx):
            forward(z, mx, mc, (mz, lax.rem(mx + d, nx), mc), slot)
            slot += 1
        forward(z, mx, mc, (mz, mx, oc), slot)
        slot += 1
    for dz in range(nz):
        z = across(mz, dz)
        for d in range(1, nx):
            x = lax.rem(mx + nx - d, nx)
            arrived(z, x, mc)
            forward(z, x, mc, (mz, mx, oc), slot)
            slot += 1
    for copy in load_recent:
        copy.wait()
    for dz in range(nz):
        z = across(mz, dz)
        for d in range(nx):
            arrived(z, lax.rem(mx + nx - d, nx), oc)

    many = min(n, 256 // slab)
    rb = many * slab
    slabs = gath.reshape(n, slab, part)

    def similar(b):
        every = slabs[pl.ds(b * many, many)].reshape(rb, part)
        group = lax.rem(lax.broadcasted_iota(jnp.int32, (rb, local_recent), 0), GROUP)
        acc = jnp.zeros((rb, local_recent), jnp.float32)
        for q in range(GROUP):
            term = lax.dot_general(
                every, recent[q * local_recent : (q + 1) * local_recent, :],
                (((1,), (1,)), ((), ())), preferred_element_type=jnp.float32,
            )
            acc = jnp.where(group == q, term, acc)
        acc = acc.reshape(rb // GROUP, GROUP, local_recent)
        sim = jnp.sum(acc, axis=1, keepdims=True) * (1.0 / math.sqrt(width))
        weights = jnp.broadcast_to(jnp.tanh(sim), acc.shape).reshape(rb, local_recent)
        for q in range(GROUP):
            wmask[pl.ds(b * rb, rb), q * local_recent : (q + 1) * local_recent] = jnp.where(
                group == q, weights, 0.0
            ).astype(jnp.bfloat16)

    def each_block(body):
        if n == many:
            body(0)
        else:
            lax.fori_loop(0, n // many, lambda b, c: (body(b), c)[1], 0)

    each_block(similar)

    cw = part // CHUNKS
    copies = []

    def start(src, dst, ss, rs, to):
        copy = pltpu.make_async_remote_copy(
            src_ref=src, dst_ref=dst, send_sem=ss, recv_sem=rs,
            device_id=flat(*to), device_id_type=MESH,
        )
        copy.start()
        copies.append(copy)
        return copy

    core_copies, x_copies, z_copies = {}, {}, {}

    def stage_core(k):
        def body(b):
            term = jnp.dot(
                wmask[pl.ds(b * rb, rb), :], recent[:, k * cw : (k + 1) * cw],
                preferred_element_type=jnp.float32,
            ).reshape(many, slab, cw)
            tf.at[k].reshape(n, slab, cw)[pl.ds(b * many, many)] = term
            tb.at[k].reshape(n, slab, cw)[pl.ds(b * many, many)] = term.astype(jnp.bfloat16)

        each_block(body)
        core_copies[k] = start(
            tb.at[k, oc], r1.at[k], c_send.at[k], c_recv.at[k], (mz, mx, oc)
        )

    def send_x(k, src, dst):
        for d in range(1, nx):
            x = lax.rem(mx + d, nx)
            x_copies[k, d] = start(
                src.at[k, x], dst.at[k, d - 1],
                x_send.at[k, d - 1], x_recv.at[k, d - 1], (mz, x, mc),
            )

    def send_z(k, src, dst):
        for d in reversed(range(1, nz)):
            z = across(mz, d)
            z_copies[k, d] = start(
                src.at[k, z], dst.at[k, d - 1],
                z_send.at[k, d - 1], z_recv.at[k, d - 1], (z, mx, mc),
            )

    def add(total, copies, k, source):
        for d in range(1, source.shape[1] + 1):
            copies[k, d].wait_recv()
            total = total + source[k, d - 1].astype(jnp.float32)
        return total

    def stage_first(k):
        core_copies[k].wait_recv()
        total = tf[k, mc] + r1[k].astype(jnp.float32)
        if k % 2:
            s1f[k] = total
            for z in range(nz):
                t1b[k // 2, z] = total[:, z].astype(jnp.bfloat16)
            for d in reversed(range(1, nz)):
                z = across(mz, d)
                z_copies[k, d] = start(
                    t1b.at[k // 2, z], t2.at[k // 2, d - 1],
                    z_send.at[k, d - 1], z_recv.at[k, d - 1], (z, mx, mc),
                )
        else:
            s1f[k] = total
            s1b[k] = total.astype(jnp.bfloat16)
            send_x(k, s1b, r2)

    def stage_second(k):
        if k % 2:
            total = s1f[k, :, mz]
            for d in range(1, nz):
                z_copies[k, d].wait_recv()
                total = total + t2[k // 2, d - 1].astype(jnp.float32)
            t2f[k // 2] = total
            t2b[k // 2] = total.astype(jnp.bfloat16)
            for d in range(1, nx):
                x = lax.rem(mx + d, nx)
                x_copies[k, d] = start(
                    t2b.at[k // 2, x], t3.at[k // 2, d - 1],
                    x_send.at[k, d - 1], x_recv.at[k, d - 1], (mz, x, mc),
                )
        else:
            total = add(s1f[k, mx], x_copies, k, r2)
            s2f[k] = total
            s2b[k] = total.astype(jnp.bfloat16)
            send_z(k, s2b, r3)

    def finish(k):
        if k % 2:
            total = t2f[k // 2, mx]
            for d in range(1, nx):
                x_copies[k, d].wait_recv()
                total = total + t3[k // 2, d - 1].astype(jnp.float32)
        else:
            total = add(s2f[k, mz], z_copies, k, r3)
        out_ref[:, k * cw : (k + 1) * cw] = (
            total * (1.0 / math.sqrt(total_recent))
        ).astype(jnp.bfloat16)

    stages = (stage_core, stage_first, stage_second, finish)
    for stage in stages:
        for k in range(CHUNKS):
            stage(k)
    for copy in sent + copies:
        copy.wait_send()


def per_device(dims, late_grads, projections, recent_sketches):
    nz, nx, nc = dims
    local_rows, items, kinds, width_in = late_grads.shape
    rank = projections.shape[1] // 4
    local_recent, width = recent_sketches.shape
    n = nz * nx * nc
    slab, part = local_rows * GROUP, width // GROUP
    bf16, f32 = jnp.bfloat16, jnp.float32
    dma = pltpu.SemaphoreType.DMA
    cw = part // CHUNKS
    sends = (nz - 1) + nz * nx + nz * (nx - 1)
    out = pl.pallas_call(
        functools.partial(kernel, dims, items, rank, local_recent * n),
        out_shape=pltpu.VMEM((slab, part), bf16),
        in_specs=[pl.BlockSpec(memory_space=pl.ANY)] * 3,
        out_specs=pl.BlockSpec(memory_space=pltpu.VMEM),
        scratch_shapes=[
            pltpu.VMEM((local_rows * items, kinds, width_in), bf16),
            pltpu.VMEM(projections.shape, bf16),
            pltpu.VMEM((GROUP * local_recent, part), bf16),
            pltpu.VMEM((nc, nx, nz, slab, part), bf16),
            pltpu.VMEM((n * slab, GROUP * local_recent), bf16),
            pltpu.VMEM((CHUNKS, nc, nx, nz, slab, cw), f32),
            pltpu.VMEM((CHUNKS, nc, nx, nz, slab, cw), bf16),
            pltpu.VMEM((CHUNKS, nx, nz, slab, cw), bf16),
            pltpu.VMEM((CHUNKS, nx, nz, slab, cw), f32),
            pltpu.VMEM((CHUNKS, nx, nz, slab, cw), bf16),
            pltpu.VMEM((CHUNKS, nx - 1, nz, slab, cw), bf16),
            pltpu.VMEM((CHUNKS, nz, slab, cw), f32),
            pltpu.VMEM((CHUNKS, nz, slab, cw), bf16),
            pltpu.VMEM((CHUNKS, nz - 1, slab, cw), bf16),
            pltpu.VMEM((CHUNKS // 2, nz, nx, slab, cw), bf16),
            pltpu.VMEM((CHUNKS // 2, nz - 1, nx, slab, cw), bf16),
            pltpu.VMEM((CHUNKS // 2, nx, slab, cw), f32),
            pltpu.VMEM((CHUNKS // 2, nx, slab, cw), bf16),
            pltpu.VMEM((CHUNKS // 2, nx - 1, slab, cw), bf16),
            dma((GROUP + 2 * LOADS,)),
            dma((sends + nz * nx,)),
            dma(dims),
            dma((CHUNKS,)),
            dma((CHUNKS,)),
            dma((CHUNKS, nx - 1)),
            dma((CHUNKS, nx - 1)),
            dma((CHUNKS, nz - 1)),
            dma((CHUNKS, nz - 1)),
        ],
        compiler_params=pltpu.CompilerParams(
            collective_id=0, has_side_effects=True, vmem_limit_bytes=60 * 1024 * 1024
        ),
    )(late_grads.reshape(local_rows * items, kinds, width_in), projections, recent_sketches)
    return out.reshape(local_rows, width)


def solution(mesh):
    n = mesh.shape["row"]
    nx = 4 if n >= 64 else 2
    dims = (n // (2 * nx), nx, 2)
    placed = (P(("groups", "row"), None, None, None), P(), P(("groups", "row"), None))
    return jax.shard_map(
        functools.partial(per_device, dims),
        mesh=mesh,
        in_specs=placed,
        out_specs=P(("groups", "row"), None),
        check_vma=False,
    )
```

```python
import functools
import math

import jax
import jax.numpy as jnp
from jax import lax
from jax.experimental import pallas as pl
from jax.experimental.pallas import tpu as pltpu
from jax.sharding import PartitionSpec as P

GROUP = 8
CHUNKS = 2
LOADS = 4
MESH = pl.DeviceIdType.MESH


def kernel(
    dims, items, rank, total_recent,
    late_hbm, proj_hbm, recent_hbm, out_ref,
    late, proj, recent, gath, wmask, tf, tb, r1, s1f, s1b, r2, s2f, s2b, r3,
    t1b, t2, t2f, t2b, t3,
    load_sem, g_send, g_recv, c_send, c_recv, x_send, x_recv, z_send, z_recv,
):
    nz, nx, nc = dims
    width = recent_hbm.shape[1]
    part = width // GROUP
    local_recent = recent_hbm.shape[0]
    slab = gath.shape[3]
    examples = slab // GROUP
    n = nz * nx * nc
    me = lax.axis_index("row")
    mc = lax.rem(me, nc)
    mx = lax.rem(lax.div(me, nc), nx)
    mz = lax.div(me, nc * nx)
    oc = 1 - mc

    def across(z, d):
        bit = 1
        while bit <= d:
            if d & bit:
                z = z + bit - 2 * bit * lax.rem(lax.div(z, bit), 2)
            bit *= 2
        return z

    def flat(z, x, c):
        return {"row": (z * nx + x) * nc + c}

    depth = late.shape[2] // LOADS
    load_inputs = []
    for i in range(LOADS):
        part_of = pl.ds(i * depth, depth)
        pair = (
            pltpu.make_async_copy(late_hbm.at[:, :, part_of], late.at[:, :, part_of], load_sem.at[GROUP + i]),
            pltpu.make_async_copy(proj_hbm.at[part_of], proj.at[part_of], load_sem.at[GROUP + LOADS + i]),
        )
        for copy in pair:
            copy.start()
        load_inputs.append(pair)

    load_recent = []
    for q in range(GROUP):
        copy = pltpu.make_async_copy(
            recent_hbm.at[:, pl.ds(q * part, part)],
            recent.at[pl.ds(q * local_recent, local_recent), :],
            load_sem.at[q],
        )
        copy.start()
        load_recent.append(copy)

    peers = [(mz, mx, oc)]
    peers += [(mz, lax.rem(mx + d, nx), mc) for d in range(1, nx)]
    peers += [(across(mz, d), mx, mc) for d in range(1, nz)]
    barrier = pltpu.get_barrier_semaphore()
    for z, x, c in peers:
        pl.semaphore_signal(barrier, inc=1, device_id=flat(z, x, c), device_id_type=MESH)

    def onehot(shape, expr):
        r = lax.broadcasted_iota(jnp.int32, shape, 0)
        c = lax.broadcasted_iota(jnp.int32, shape, 1)
        return jnp.where(expr(r, c), 1.0, 0.0).astype(jnp.bfloat16)

    pairs = examples * items
    pick = onehot((pairs, 4 * pairs), lambda r, c: r == lax.shift_right_logical(c, 2))
    spread = onehot((rank, part), lambda r, c: r == lax.rem(c, rank))
    repeat = onehot((rank, rank * rank), lambda r, c: r == lax.div(c, rank))

    full = jnp.zeros((4 * pairs, 4 * rank), jnp.float32)
    for i, pair in enumerate(load_inputs):
        for copy in pair:
            copy.wait()
        rows = late[:, :, i * depth : (i + 1) * depth].reshape(4 * pairs, depth)
        full = full + jnp.dot(
            rows, proj[i * depth : (i + 1) * depth, :], preferred_element_type=jnp.float32
        )
    kind = lax.rem(lax.broadcasted_iota(jnp.int32, full.shape, 0), 4)
    block = lax.div(lax.broadcasted_iota(jnp.int32, full.shape, 1), rank)
    full = jnp.where(kind == block, full, 0.0).astype(jnp.bfloat16)
    factors = jnp.dot(pick, full, preferred_element_type=jnp.float32)
    sketch = jnp.zeros((slab, part), jnp.float32)
    row = lax.broadcasted_iota(jnp.int32, (slab, part), 0)
    quarter = GROUP // 2
    for layer in range(2):
        right = factors[:, 2 * layer * rank : (2 * layer + 1) * rank].astype(jnp.bfloat16)
        left = factors[:, (2 * layer + 1) * rank : (2 * layer + 2) * rank].astype(jnp.bfloat16)
        tiled = jnp.dot(right, spread, preferred_element_type=jnp.float32)
        for q in range(quarter):
            wide = jnp.dot(
                left, repeat[:, q * part : (q + 1) * part], preferred_element_type=jnp.float32
            )
            outer = wide * tiled
            for e in range(examples):
                total = jnp.sum(outer[e * items : (e + 1) * items], axis=0, keepdims=True)
                at = e * GROUP + layer * quarter + q
                sketch = jnp.where(row == at, total, sketch)
    gath[mc, mx, mz] = (sketch * (1.0 / math.sqrt(items))).astype(jnp.bfloat16)

    pl.semaphore_wait(barrier, len(peers))

    sent = []

    def forward(z, x, c, to, slot):
        copy = pltpu.make_async_remote_copy(
            src_ref=gath.at[c, x, z], dst_ref=gath.at[c, x, z],
            send_sem=g_send.at[slot], recv_sem=g_recv.at[z, x, c],
            device_id=flat(*to), device_id_type=MESH,
        )
        copy.start()
        sent.append(copy)

    def arrived(z, x, c):
        pltpu.make_async_remote_copy(
            src_ref=gath.at[c, x, z], dst_ref=gath.at[c, x, z],
            send_sem=g_send.at[0], recv_sem=g_recv.at[z, x, c],
            device_id=flat(mz, mx, oc), device_id_type=MESH,
        ).wait_recv()

    slot = 0
    for d in range(1, nz):
        forward(mz, mx, mc, (across(mz, d), mx, mc), slot)
        slot += 1
    for dz in range(nz):
        z = across(mz, dz)
        if dz:
            arrived(z, mx, mc)
        for d in range(1, nx):
            forward(z, mx, mc, (mz, lax.rem(mx + d, nx), mc), slot)
            slot += 1
        forward(z, mx, mc, (mz, mx, oc), slot)
        slot += 1
    for dz in range(nz):
        z = across(mz, dz)
        for d in range(1, nx):
            x = lax.rem(mx + nx - d, nx)
            arrived(z, x, mc)
            forward(z, x, mc, (mz, mx, oc), slot)
            slot += 1
    for copy in load_recent:
        copy.wait()
    for dz in range(nz):
        z = across(mz, dz)
        for d in range(nx):
            arrived(z, lax.rem(mx + nx - d, nx), oc)

    many = min(n, 256 // slab)
    rb = many * slab
    slabs = gath.reshape(n, slab, part)

    def similar(b):
        every = slabs[pl.ds(b * many, many)].reshape(rb, part)
        group = lax.rem(lax.broadcasted_iota(jnp.int32, (rb, local_recent), 0), GROUP)
        acc = jnp.zeros((rb, local_recent), jnp.float32)
        for q in range(GROUP):
            term = lax.dot_general(
                every, recent[q * local_recent : (q + 1) * local_recent, :],
                (((1,), (1,)), ((), ())), preferred_element_type=jnp.float32,
            )
            acc = jnp.where(group == q, term, acc)
        acc = acc.reshape(rb // GROUP, GROUP, local_recent)
        sim = jnp.sum(acc, axis=1, keepdims=True) * (1.0 / math.sqrt(width))
        weights = jnp.broadcast_to(jnp.tanh(sim), acc.shape).reshape(rb, local_recent)
        for q in range(GROUP):
            wmask[pl.ds(b * rb, rb), q * local_recent : (q + 1) * local_recent] = jnp.where(
                group == q, weights, 0.0
            ).astype(jnp.bfloat16)

    def each_block(body):
        if n == many:
            body(0)
        else:
            lax.fori_loop(0, n // many, lambda b, c: (body(b), c)[1], 0)

    each_block(similar)

    cw = part // CHUNKS
    copies = []

    def start(src, dst, ss, rs, to):
        copy = pltpu.make_async_remote_copy(
            src_ref=src, dst_ref=dst, send_sem=ss, recv_sem=rs,
            device_id=flat(*to), device_id_type=MESH,
        )
        copy.start()
        copies.append(copy)
        return copy

    core_copies, x_copies, z_copies = {}, {}, {}

    def stage_core(k):
        def body(b):
            term = jnp.dot(
                wmask[pl.ds(b * rb, rb), :], recent[:, k * cw : (k + 1) * cw],
                preferred_element_type=jnp.float32,
            ).reshape(many, slab, cw)
            tf.at[k].reshape(n, slab, cw)[pl.ds(b * many, many)] = term
            tb.at[k].reshape(n, slab, cw)[pl.ds(b * many, many)] = term.astype(jnp.bfloat16)

        each_block(body)
        core_copies[k] = start(
            tb.at[k, oc], r1.at[k], c_send.at[k], c_recv.at[k], (mz, mx, oc)
        )

    def send_x(k, src, dst):
        for d in range(1, nx):
            x = lax.rem(mx + d, nx)
            x_copies[k, d] = start(
                src.at[k, x], dst.at[k, d - 1],
                x_send.at[k, d - 1], x_recv.at[k, d - 1], (mz, x, mc),
            )

    def send_z(k, src, dst):
        for d in reversed(range(1, nz)):
            z = across(mz, d)
            z_copies[k, d] = start(
                src.at[k, z], dst.at[k, d - 1],
                z_send.at[k, d - 1], z_recv.at[k, d - 1], (z, mx, mc),
            )

    def add(total, copies, k, source):
        for d in range(1, source.shape[1] + 1):
            copies[k, d].wait_recv()
            total = total + source[k, d - 1].astype(jnp.float32)
        return total

    def stage_first(k):
        core_copies[k].wait_recv()
        total = tf[k, mc] + r1[k].astype(jnp.float32)
        if k % 2:
            s1f[k] = total
            for z in range(nz):
                t1b[k // 2, z] = total[:, z].astype(jnp.bfloat16)
            for d in reversed(range(1, nz)):
                z = across(mz, d)
                z_copies[k, d] = start(
                    t1b.at[k // 2, z], t2.at[k // 2, d - 1],
                    z_send.at[k, d - 1], z_recv.at[k, d - 1], (z, mx, mc),
                )
        else:
            s1f[k] = total
            s1b[k] = total.astype(jnp.bfloat16)
            send_x(k, s1b, r2)

    def stage_second(k):
        if k % 2:
            total = s1f[k, :, mz]
            for d in range(1, nz):
                z_copies[k, d].wait_recv()
                total = total + t2[k // 2, d - 1].astype(jnp.float32)
            t2f[k // 2] = total
            t2b[k // 2] = total.astype(jnp.bfloat16)
            for d in range(1, nx):
                x = lax.rem(mx + d, nx)
                x_copies[k, d] = start(
                    t2b.at[k // 2, x], t3.at[k // 2, d - 1],
                    x_send.at[k, d - 1], x_recv.at[k, d - 1], (mz, x, mc),
                )
        else:
            total = add(s1f[k, mx], x_copies, k, r2)
            s2f[k] = total
            s2b[k] = total.astype(jnp.bfloat16)
            send_z(k, s2b, r3)

    def finish(k):
        if k % 2:
            total = t2f[k // 2, mx]
            for d in range(1, nx):
                x_copies[k, d].wait_recv()
                total = total + t3[k // 2, d - 1].astype(jnp.float32)
        else:
            total = add(s2f[k, mz], z_copies, k, r3)
        out_ref[:, k * cw : (k + 1) * cw] = (
            total * (1.0 / math.sqrt(total_recent))
        ).astype(jnp.bfloat16)

    stages = (stage_core, stage_first, stage_second, finish)
    for stage in stages:
        for k in range(CHUNKS):
            stage(k)
    for copy in sent + copies:
        copy.wait_send()


def per_device(dims, late_grads, projections, recent_sketches):
    nz, nx, nc = dims
    local_rows, items, kinds, width_in = late_grads.shape
    rank = projections.shape[1] // 4
    local_recent, width = recent_sketches.shape
    n = nz * nx * nc
    slab, part = local_rows * GROUP, width // GROUP
    bf16, f32 = jnp.bfloat16, jnp.float32
    dma = pltpu.SemaphoreType.DMA
    cw = part // CHUNKS
    sends = (nz - 1) + nz * nx + nz * (nx - 1)
    out = pl.pallas_call(
        functools.partial(kernel, dims, items, rank, local_recent * n),
        out_shape=pltpu.VMEM((slab, part), bf16),
        in_specs=[pl.BlockSpec(memory_space=pl.ANY)] * 3,
        out_specs=pl.BlockSpec(memory_space=pltpu.VMEM),
        scratch_shapes=[
            pltpu.VMEM((local_rows * items, kinds, width_in), bf16),
            pltpu.VMEM(projections.shape, bf16),
            pltpu.VMEM((GROUP * local_recent, part), bf16),
            pltpu.VMEM((nc, nx, nz, slab, part), bf16),
            pltpu.VMEM((n * slab, GROUP * local_recent), bf16),
            pltpu.VMEM((CHUNKS, nc, nx, nz, slab, cw), f32),
            pltpu.VMEM((CHUNKS, nc, nx, nz, slab, cw), bf16),
            pltpu.VMEM((CHUNKS, nx, nz, slab, cw), bf16),
            pltpu.VMEM((CHUNKS, nx, nz, slab, cw), f32),
            pltpu.VMEM((CHUNKS, nx, nz, slab, cw), bf16),
            pltpu.VMEM((CHUNKS, nx - 1, nz, slab, cw), bf16),
            pltpu.VMEM((CHUNKS, nz, slab, cw), f32),
            pltpu.VMEM((CHUNKS, nz, slab, cw), bf16),
            pltpu.VMEM((CHUNKS, nz - 1, slab, cw), bf16),
            pltpu.VMEM((CHUNKS // 2, nz, nx, slab, cw), bf16),
            pltpu.VMEM((CHUNKS // 2, nz - 1, nx, slab, cw), bf16),
            pltpu.VMEM((CHUNKS // 2, nx, slab, cw), f32),
            pltpu.VMEM((CHUNKS // 2, nx, slab, cw), bf16),
            pltpu.VMEM((CHUNKS // 2, nx - 1, slab, cw), bf16),
            dma((GROUP + 2 * LOADS,)),
            dma((sends + nz * nx,)),
            dma(dims),
            dma((CHUNKS,)),
            dma((CHUNKS,)),
            dma((CHUNKS, nx - 1)),
            dma((CHUNKS, nx - 1)),
            dma((CHUNKS, nz - 1)),
            dma((CHUNKS, nz - 1)),
        ],
        compiler_params=pltpu.CompilerParams(
            collective_id=0, has_side_effects=True, vmem_limit_bytes=60 * 1024 * 1024
        ),
    )(late_grads.reshape(local_rows * items, kinds, width_in), projections, recent_sketches)
    return out.reshape(local_rows, width)


def solution(mesh):
    n = mesh.shape["row"]
    nx = 4 if n >= 64 else 2
    dims = (n // (2 * nx), nx, 2)
    placed = (P(("groups", "row"), None, None, None), P(), P(("groups", "row"), None))
    return jax.shard_map(
        functools.partial(per_device, dims),
        mesh=mesh,
        in_specs=placed,
        out_specs=P(("groups", "row"), None),
        check_vma=False,
    )
```
